256 devices in a mesh: ctx: 32 (over z, x), ch: 8 (over y, core).
Axes of the slice: x: 4, y: 4, z: 8, core: 2. Of those that a mesh axis runs over, the one named last changes fastest.
Arguments:
- query_input: bfloat16 [4096, 4096], P('ctx', 'ch'), may hold values from -6 to 6
- key_input: bfloat16 [4096, 4096], P('ctx', 'ch'), may hold values from -6 to 6
- value_input: bfloat16 [4096, 4096], P('ctx', 'ch'), may hold values from -6 to 6
- short_weight: float32 [3, 3, 4096], P(None, None, 'ch'), may hold values from -3.5 to 3.5
- residue: float32 [16, 4096], P(None, 'ch'), may hold values from -1.5 to 1.5
- decay_rate: float32 [16, 4096], P(None, 'ch'), may hold values from 0.00012207031 to 0.05
- skip_gain: float32 [4096], P('ch'), may hold values from -1 to 1
- out_weight: bfloat16 [4096, 8192], P('ch'), may hold values from -0.125 to 0.125
Outputs:
- layer_output: bfloat16 [4096, 8192], P('ctx', 'ch')
The draws below stay inside these ranges and needn't reach their ends.
All inputs are finite; a program needn't handle non-finite values.
Results may differ from the reference program's by a relative error of at most 0.015.
Values may be sent and summed in bfloat16 or wider, within the bound.
No kernel may reach another device: no remote copies, remote signals or barrier semaphores. Data moves between devices by JAX's collectives and lax.ppermute only.
A program may use at most 64 MiB of HBM per device.

```python
import math
import jax
import jax.numpy as jnp

D = 8192
DH = 4096
ORDER = 16
TAPS = 3
TOKENS = 4096


def spiked(entries, key, source, target, parts, factor):
    owner, partner = [(jnp.arange(entries.shape[position]) // (entries.shape[position] // parts)).reshape([-1 if axis == position else 1 for axis in range(entries.ndim)]) for position in (source, target)]
    chosen = jax.random.permutation(key, parts)[partner]
    strong = (owner == chosen) | (owner == (partner + parts // 2) % parts)
    return jnp.where(strong, factor * entries, entries)


def block_scale(key, shape, pieces, smallest, largest):
    loudness = 1.0
    for axis_at, shards_of in pieces:
        heights = jax.random.uniform(jax.random.fold_in(jax.random.fold_in(key, 6), axis_at), (shards_of,), jnp.float32, smallest / len(pieces), largest / len(pieces))
        loudness = loudness * jnp.repeat(jnp.exp(heights), shape[axis_at] // shards_of).reshape((-1,) + (1,) * (len(shape) - 1 - axis_at))
    return loudness


def normal_values(stream_key, extent, spread, reach, pieces=(), held_as=jnp.bfloat16):
    gain = block_scale(stream_key, extent, pieces, -0.22, 0.18) if pieces else 1.0
    array = jax.random.normal(stream_key, extent, jnp.float32) * spread * gain
    return jnp.minimum(jnp.maximum(array, -reach), reach).astype(held_as)


def gaussian_with(stream_key, extent, scale, most, split, heavy, kind=jnp.bfloat16):
    drawn = scale * jax.random.normal(stream_key, extent, jnp.float32)
    if split:
        drawn = drawn * block_scale(stream_key, extent, split, -0.22, 0.18)
    return jnp.clip(spiked(drawn, jax.random.fold_in(stream_key, 3), *heavy), -most, most).astype(kind)


def setup_inputs(seed: int = 0) -> dict:
    arg_keys = jax.random.split(jax.random.key(seed), 9)
    return {
        "query_input": normal_values(arg_keys[0], (TOKENS, DH), 1.0, 6.0, ((0, 32), (1, 8))),
        "key_input": normal_values(arg_keys[1], (TOKENS, DH), 1.0, 6.0, ((0, 32), (1, 8))),
        "value_input": normal_values(arg_keys[2], (TOKENS, DH), 1.0, 6.0, ((0, 32), (1, 8))),
        "short_weight": normal_values(arg_keys[3], (3, TAPS, DH), TAPS ** -0.5, 3.5, ((2, 8),), jnp.float32),
        "residue": normal_values(arg_keys[4], (ORDER, DH), 0.25, 1.5, ((1, 8),), jnp.float32),
        "decay_rate": jnp.clip(jnp.exp(math.log(0.05) - 6.015181 * jax.random.uniform(arg_keys[5], (ORDER, DH), jnp.float32) ** block_scale(arg_keys[5], (ORDER, DH), ((1, 8),), -0.2, 0.2)), 0.00012207031, 0.05),
        "skip_gain": jnp.clip(jax.random.uniform(arg_keys[6], (DH,), jnp.float32, -1.0, 1.0) * block_scale(arg_keys[6], (DH,), ((0, 8),), -0.4, 0.0), -1.0, 1.0),
        "out_weight": gaussian_with(arg_keys[7], (DH, D), DH ** -0.5, 0.125, ((0, 8),), (0, 1, 8, 2.0)),
    }


def filter_block(residue, decay_rate, first_row, row_count):
    moments = (first_row + jnp.arange(row_count, dtype=jnp.int32)).astype(jnp.float32)[:, None]
    running = jnp.zeros((row_count, residue.shape[1]), jnp.float32)
    for order_mode in range(residue.shape[0]):
        running = running + residue[order_mode] * jnp.sqrt(2.0 * decay_rate[order_mode]) * jnp.exp(-decay_rate[order_mode] * moments)
    return running

def short_filter(raw_rows, prior_rows, taps):
    extended = jnp.concatenate([prior_rows, raw_rows], axis=0).astype(jnp.float32)
    length_rows = raw_rows.shape[0]
    tap_count = taps.shape[0]
    running = jnp.zeros(raw_rows.shape, jnp.float32)
    for offset in range(tap_count):
        running = running + taps[offset] * extended[tap_count - 1 - offset:tap_count - 1 - offset + length_rows]
    return running

def reference(query_input, key_input, value_input, short_weight, residue, decay_rate, skip_gain, out_weight):
    prior_zero = jnp.zeros((TAPS - 1, DH), jnp.bfloat16)
    query_conv = short_filter(query_input, prior_zero, short_weight[0])
    key_conv = short_filter(key_input, prior_zero, short_weight[1])
    value_conv = short_filter(value_input, prior_zero, short_weight[2])
    mixed_input = key_conv * value_conv
    impulse = filter_block(residue, decay_rate, 0, TOKENS)
    spectrum = jnp.fft.rfft(mixed_input, n=2 * TOKENS, axis=0) * jnp.fft.rfft(impulse, n=2 * TOKENS, axis=0)
    convolved = jnp.fft.irfft(spectrum, n=2 * TOKENS, axis=0)[:TOKENS].astype(jnp.float32)
    gated = (query_conv * (convolved + skip_gain * mixed_input)).astype(jnp.bfloat16)
    return jnp.dot(gated, out_weight, preferred_element_type=jnp.float32).astype(jnp.bfloat16)
```

```python
import functools

import jax
import jax.numpy as jnp
from jax import lax
from jax.experimental import pallas as pl
from jax.experimental.pallas import tpu as pltpu
from jax.sharding import PartitionSpec as P

F32 = jnp.float32
BF16 = jnp.bfloat16
ROWS = 8
LANES = 128
REDUCE = "a2a"
ZSTAGE = "perm"


def edge_kernel(q_ref, k_ref, v_ref, out_ref):
    out_ref[...] = jnp.concatenate([r[...].astype(F32) for r in (q_ref, k_ref, v_ref)], axis=0)


def edge_rows(q, k, v):
    rows, width = q.shape
    spec = pl.BlockSpec((16, width), lambda i: (rows // 16 - 1, 0))
    return pl.pallas_call(
        edge_kernel,
        grid=(1,),
        in_specs=[spec] * 3,
        out_specs=pl.BlockSpec((48, width), lambda i: (0, 0)),
        out_shape=jax.ShapeDtypeStruct((48, width), F32),
        name="edge",
    )(q, k, v)


def short_filter(x, earlier, taps):
    row = lax.broadcasted_iota(jnp.int32, x.shape, 0)
    one = jnp.where(row == 0, earlier[15:16], pltpu.roll(x, 1, 0))
    two = jnp.where(row == 0, earlier[14:15], jnp.where(row == 1, earlier[15:16], pltpu.roll(x, 2, 0)))
    return taps[0:1] * x + taps[1:2] * one + taps[2:3] * two


def state_kernel(q_ref, k_ref, v_ref, e_ref, w_ref, d_ref, query_ref, mixed_ref, state_ref):
    query_ref[...] = short_filter(q_ref[...].astype(F32), e_ref[0:16], w_ref[0])
    keys = short_filter(k_ref[...].astype(F32), e_ref[16:32], w_ref[1])
    values = short_filter(v_ref[...].astype(F32), e_ref[32:48], w_ref[2])
    mixed_ref[...] = keys * values
    rate = d_ref[...]
    order = rate.shape[0]
    fall = jnp.exp(-float(ROWS) * rate)
    falls = [jnp.broadcast_to(fall[r : r + 1], (ROWS, LANES)) for r in range(order)]
    sums = [jnp.zeros((ROWS, LANES), F32) for _ in range(order)]
    for i in range(mixed_ref.shape[0] // ROWS):
        tile = mixed_ref[i * ROWS : (i + 1) * ROWS]
        sums = [s * f + tile for s, f in zip(sums, falls)]
    left = (ROWS - 1 - lax.broadcasted_iota(jnp.int32, (ROWS, LANES), 0)).astype(F32)
    for r in range(order):
        weighed = sums[r] * jnp.exp(-rate[r : r + 1] * left)
        state_ref[r : r + 1] = jnp.sum(weighed, axis=0, keepdims=True)


def lane_spec(shape):
    lead = len(shape) - 1
    return pl.BlockSpec(tuple(shape[:-1]) + (LANES,), lambda i: (0,) * lead + (i,))


def lane_call(kernel, arrays, outs, name, scratch=(), flops=10**7):
    width = arrays[0].shape[-1]
    return pl.pallas_call(
        kernel,
        grid=(width // LANES,),
        in_specs=[lane_spec(a.shape) for a in arrays],
        out_specs=[lane_spec(o) for o in outs],
        out_shape=[jax.ShapeDtypeStruct(o, F32) for o in outs],
        scratch_shapes=list(scratch),
        cost_estimate=pl.CostEstimate(flops=flops, bytes_accessed=10**6, transcendentals=10**5),
        name=name,
    )(*arrays)


def local_kernel(mixed_ref, res_ref, d_ref, skip_ref, out_ref, impulse_ref):
    rate = d_ref[...]
    order = rate.shape[0]
    tiles = mixed_ref.shape[0] // ROWS
    size = res_ref[...] * jnp.sqrt(2.0 * rate)
    fall = jnp.exp(-float(ROWS) * rate)
    row = lax.broadcasted_iota(jnp.int32, (ROWS, LANES), 0).astype(F32)
    modes = [size[r : r + 1] * jnp.exp(-rate[r : r + 1] * row) for r in range(order)]
    falls = [jnp.broadcast_to(fall[r : r + 1], (ROWS, LANES)) for r in range(order)]
    for m in range(tiles):
        impulse_ref[m * ROWS : (m + 1) * ROWS] = sum(modes[1:], modes[0])
        modes = [a * f for a, f in zip(modes, falls)]
    skip = jnp.broadcast_to(skip_ref[...], (ROWS, LANES))
    mixed = mixed_ref[...]
    position = lax.broadcasted_iota(jnp.int32, mixed.shape, 0)
    for j in range(ROWS):
        moved = mixed if j == 0 else jnp.where(position < j, 0.0, pltpu.roll(mixed, j, 0))
        pieces = [moved[i * ROWS : (i + 1) * ROWS] for i in range(tiles)]
        if j == 0:
            sums = [skip * piece for piece in pieces]
        else:
            sums = [out_ref[i * ROWS : (i + 1) * ROWS] for i in range(tiles)]
        for m in range(tiles):
            weight = jnp.broadcast_to(impulse_ref[m * ROWS + j : m * ROWS + j + 1], (ROWS, LANES))
            for i in range(m, tiles):
                sums[i] = sums[i] + weight * pieces[i - m]
        for i in range(tiles):
            out_ref[i * ROWS : (i + 1) * ROWS] = sums[i]


def group_kernel(span, own_ref, r1_ref, r2_ref, r3_ref, d_ref, total_ref, before_ref):
    x = lax.axis_index("ctx") % 4
    rate = d_ref[...] * float(span)
    total = own_ref[...] * jnp.exp(-rate * (3 - x).astype(F32))
    before = jnp.zeros_like(total)
    for d, ref in ((1, r1_ref), (2, r2_ref), (3, r3_ref)):
        source = (x + 4 - d) % 4
        got = ref[...]
        total = total + got * jnp.exp(-rate * (3 - source).astype(F32))
        before = before + jnp.where(x >= d, got * jnp.exp(-rate * float(d - 1)), 0.0)
    total_ref[...] = total
    before_ref[...] = before


def gate_kernel(span, query_ref, local_ref, before_ref, res_ref, d_ref, *rest):
    *far, out_ref = rest
    x = (lax.axis_index("ctx") % 4).astype(F32)
    rate = d_ref[...]
    order = rate.shape[0]
    step = jnp.exp(-rate * float(4 * span))
    carried = far[-1][...]
    for ref in far[-2::-1]:
        carried = carried * step + ref[...]
    carry = before_ref[...] + carried * jnp.exp(-rate * (span * x))
    carry = carry * res_ref[...] * jnp.sqrt(2.0 * rate)
    fall = jnp.exp(-float(ROWS) * rate)
    row = lax.broadcasted_iota(jnp.int32, (ROWS, LANES), 0).astype(F32) + 1.0
    modes = [carry[r : r + 1] * jnp.exp(-rate[r : r + 1] * row) for r in range(order)]
    falls = [jnp.broadcast_to(fall[r : r + 1], (ROWS, LANES)) for r in range(order)]
    for i in range(span // ROWS):
        at = slice(i * ROWS, (i + 1) * ROWS)
        total = local_ref[at] + sum(modes[1:], modes[0])
        out_ref[at] = query_ref[at] * total
        modes = [a * f for a, f in zip(modes, falls)]


def project_kernel(gated_ref, w_ref, out_ref):
    out_ref[0] = jnp.dot(gated_ref[...].astype(BF16), w_ref[...], preferred_element_type=F32).astype(BF16)


def project(gated, weight, parts):
    rows, depth = gated.shape
    width = weight.shape[1] // parts
    return pl.pallas_call(
        project_kernel,
        grid=(parts,),
        in_specs=[
            pl.BlockSpec((rows, depth), lambda i: (0, 0)),
            pl.BlockSpec((depth, width), lambda i: (0, i)),
        ],
        out_specs=pl.BlockSpec((1, rows, width), lambda i: (i, 0, 0)),
        out_shape=jax.ShapeDtypeStruct((parts, rows, width), BF16),
        name="project",
    )(gated, weight)


def piece_kernel(at_ref, gated_ref, w_ref, out_ref):
    out_ref[...] = jnp.dot(gated_ref[...].astype(BF16), w_ref[...], preferred_element_type=F32).astype(BF16)


def piece(gated, weight, parts, at):
    rows, depth = gated.shape
    width = weight.shape[1] // parts
    return pl.pallas_call(
        piece_kernel,
        grid_spec=pltpu.PrefetchScalarGridSpec(
            num_scalar_prefetch=1,
            grid=(2,),
            in_specs=[
                pl.BlockSpec((rows, depth), lambda i, at: (0, 0)),
                pl.BlockSpec((depth, width // 2), lambda i, at: (0, 2 * at[0] + i)),
            ],
            out_specs=pl.BlockSpec((rows, width // 2), lambda i, at: (0, i)),
        ),
        out_shape=jax.ShapeDtypeStruct((rows, width), BF16),
        cost_estimate=pl.CostEstimate(flops=2 * rows * depth * width, bytes_accessed=2 * depth * width, transcendentals=0),
        name="piece",
    )(at, gated, weight)


def reduce_parts(gated, weight):
    parts = lax.axis_size("ch")
    if REDUCE == "perm":
        me = lax.axis_index("ch")
        got = []
        for d in (4, 3, 5, 2, 6, 7, 1):
            mine = piece(gated, weight, parts, ((me + d) % parts).astype(jnp.int32).reshape(1))
            pairs = [(i, (i + d) % parts) for i in range(parts)]
            got.append(lax.ppermute(mine, "ch", pairs))
        total = piece(gated, weight, parts, me.astype(jnp.int32).reshape(1)).astype(F32)
        for one in got:
            total = total + one.astype(F32)
        return total.astype(BF16)
    partial = project(gated, weight, parts)
    if REDUCE == "a2a":
        got = lax.all_to_all(partial, "ch", 0, 0, tiled=True)
        return jnp.sum(got.astype(F32), axis=0).astype(BF16)
    return lax.psum_scatter(partial, "ch", scatter_dimension=0, tiled=False)


def body(query_input, key_input, value_input, short_weight, residue, decay_rate, skip_gain, out_weight):
    count = lax.axis_size("ctx")
    rows, width = query_input.shape
    order = residue.shape[0]
    edge = edge_rows(query_input, key_input, value_input)
    edge = lax.ppermute(edge, "ctx", [(i, i + 1) for i in range(count - 1)])
    query, mixed, state = lane_call(
        state_kernel,
        [query_input, key_input, value_input, edge, short_weight, decay_rate],
        [(rows, width), (rows, width), (order, width)],
        "state",
    )
    near = []
    for d in (1, 2, 3):
        pairs = [(4 * z + x, 4 * z + (x + d) % 4) for z in range(count // 4) for x in range(4)]
        near.append(lax.ppermute(state, "ctx", pairs))
    (local,) = lane_call(
        local_kernel,
        [mixed, residue, decay_rate, skip_gain[None, :]],
        [(rows, width)],
        "local",
        scratch=[pltpu.VMEM((rows, LANES), F32)],
        flops=10**9,
    )
    total, before = lane_call(
        functools.partial(group_kernel, rows),
        [state, *near, decay_rate],
        [(order, width), (order, width)],
        "group",
    )
    far = []
    for d in range(1, count // 4):
        pairs = [(i, i + 4 * d) for i in range(count - 4 * d)]
        far.append(lax.ppermute(total, "ctx", pairs))
    (gated,) = lane_call(
        functools.partial(gate_kernel, rows),
        [query, local, before, residue, decay_rate, *far],
        [(rows, width)],
        "gate",
    )
    return reduce_parts(gated, out_weight)


def solution(mesh):
    return jax.shard_map(
        body,
        mesh=mesh,
        in_specs=(
            P("ctx", "ch"),
            P("ctx", "ch"),
            P("ctx", "ch"),
            P(None, None, "ch"),
            P(None, "ch"),
            P(None, "ch"),
            P("ch"),
            P("ch", None),
        ),
        out_specs=P("ctx", "ch"),
        check_vma=False,
    )
```
